1024 devices in a mesh: dp: 32 (over y, x), expert: 32 (over z, core).
Axes of the slice: x: 4, y: 8, z: 16, core: 2. Of those that a mesh axis runs over, the one named last changes fastest.
Arguments:
- grad_out: bfloat16 [131072, 2048], P(('dp', 'expert')), may hold values from -6 to 6
- probs: bfloat16 [131072, 2], P(('dp', 'expert')), may hold values from 0.019897461 to 0.5
- routes: int32 [131072, 2], P(('dp', 'expert')), may hold values from 0 to 31, all different within a row; in each aligned block of 128 rows (0 to 127, 128 to 255, ...) at most 12 rows name the same one
- saved_gate: bfloat16 [32, 32, 32, 12, 768], P('dp', 'expert'), may hold values from -6 to 6
- saved_up: bfloat16 [32, 32, 32, 12, 768], P('dp', 'expert'), may hold values from -6 to 6
- w_down: bfloat16 [32, 768, 2048], P('expert'), may hold values from -0.21875 to 0.21875
Outputs:
- grad_gate: bfloat16 [32, 32, 32, 12, 768], P('dp', 'expert')
- grad_up: bfloat16 [32, 32, 32, 12, 768], P('dp', 'expert')
- grad_weight: float32 [32, 768, 2048], P('expert', 'dp')
- route_grad: float32 [131072, 2], P(('dp', 'expert'))
The draws below stay inside these ranges and needn't reach their ends.
Inputs may be any that keep to these rules, and one draw needn't show every extreme that they name: A token's 2 routes name different experts. Among one device's 128 tokens no expert is named by more than 12 routes, a bound that some block reaches.
All inputs are finite; a program needn't handle non-finite values.
Results may differ from the reference program's by a relative error of at most 0.0049.
Values may be sent and summed in bfloat16 or wider, within the bound.
A program may use at most 64 MiB of HBM per device.

```python
import math
import jax
import jax.numpy as jnp
import numpy as np
from jax import lax

D = 2048
FF = 768
TOP = 2
TOK_DEV = 128
EXPERTS = 32
CAP = 12
TOKENS = 131072
N_DP = 32
N_EXPERT = 32


def levels(rng, dims, split, least, high):
    def one(dim, shards_of):
        draws = jax.random.uniform(jax.random.fold_in(jax.random.fold_in(rng, 6), dim), (shards_of,), jnp.float32, least / len(split), high / len(split))
        return jnp.repeat(jnp.exp(draws), dims[dim] // shards_of).reshape((-1,) + (1,) * (len(dims) - dim - 1))

    loudness = one(*split[0])
    for cut in split[1:]:
        loudness = loudness * one(*cut)
    return loudness


def routed_block(own_key, own, number, rows, count, top, limit, skew):
    ranking = jax.random.permutation(own_key, count)
    crowded, usual = load_shares(count, rows * top, limit, skew, True), load_shares(count, rows * top, limit, skew, False)
    places = jnp.arange(count)

    def named(sizes, rotation):
        used = int((sizes > 0).sum())
        fixed = max(1, used // 4)
        passed = fixed + (places - fixed + rotation * (used - fixed)) % max(1, count - fixed)
        return jnp.zeros((count,), jnp.int32).at[ranking[jnp.where(places < fixed, places, passed)]].set(jnp.asarray(sizes, jnp.int32))

    sizes = jnp.where(number % 4 == 0, named(crowded, number // 4), named(usual, number - number // 4 - 1))
    mixed = jax.random.permutation(jax.random.fold_in(own, 3), count)
    source_of, receiver = mixed[0:count // 2 * 2:2], mixed[1:count // 2 * 2:2]
    margin = jnp.minimum(sizes[source_of] - 1, limit - sizes[receiver]) // 2
    margin = jnp.where((source_of == ranking[0]) | (receiver == ranking[0]) | (sizes[receiver] == 0), 0, jnp.maximum(margin, 0))
    passed = jax.random.randint(jax.random.fold_in(own, 4), (count // 2,), 0, 1 << 20) % (margin + 1)
    sizes = sizes.at[source_of].add(-passed).at[receiver].add(passed)
    members = jnp.searchsorted(jnp.cumsum(sizes), jnp.arange(rows * top), side="right").astype(jnp.int32)
    table = members.reshape(top, rows).T
    table = table[jax.random.permutation(jax.random.fold_in(own, 1), rows)]
    rotation = jax.random.randint(jax.random.fold_in(own, 2), (rows, 1), 0, top)
    return jnp.take_along_axis(table, (jnp.arange(top)[None, :] + rotation) % top, axis=1)


def load_shares(amount, total, reach, slope, full):
    weights = [(1 << 20) // math.isqrt(grade ** slope) + 1 for grade in range(1, amount + 1)]
    largest = reach if full else min(reach, max(-(-total // amount), total * weights[0] // sum(weights)))
    least = 1 if total - largest >= amount - 1 else 0
    holding, spare = [largest] + [least] * (amount - 1), total - largest - least * (amount - 1)
    while spare > 0:
        candidates = [i for i in range(1, amount) if holding[i] < largest] or [i for i in range(1, amount) if holding[i] < reach]
        pool, left = sum([weights[i] for i in candidates]), spare
        for i in candidates:
            more = min(reach - holding[i], max(1, left * weights[i] // pool), spare)
            holding[i] = holding[i] + more
            spare = spare - more
    return np.array(holding)


def normal_values(own_key, extent, deviation, limit, split=(), kind=jnp.bfloat16):
    drawn = jax.random.normal(own_key, extent, jnp.float32) * deviation
    if len(split) > 0:
        drawn = levels(own_key, extent, split, -0.22, 0.18) * drawn
    return jnp.clip(drawn, min=-limit, max=limit).astype(kind)


def setup_inputs(seed: int = 0) -> dict:
    splits = jax.random.split(jax.random.key(seed), 7)
    grad_out = normal_values(splits[0], (TOKENS, D), 1.0, 6.0, ((0, 1024),))
    probs = jnp.clip(jnp.exp(math.log(0.5) - 3.224016 * jax.random.uniform(splits[1], (TOKENS, TOP), jnp.float32) ** levels(splits[1], (TOKENS, TOP), ((0, 1024),), -0.2, 0.2)), 0.019897461, 0.5).astype(jnp.bfloat16)
    routes_keys = jax.random.split(jax.random.fold_in(splits[2], 1), TOKENS // TOK_DEV)
    routes_turns = jax.random.permutation(jax.random.fold_in(splits[2], 3), TOKENS // TOK_DEV)
    routes = jax.vmap(lambda own, number: routed_block(jax.random.fold_in(splits[2], 2), own, number, TOK_DEV, EXPERTS, TOP, CAP, 2))(routes_keys, routes_turns).reshape((TOKENS, TOP))
    saved_gate = normal_values(splits[3], (N_DP, EXPERTS, N_EXPERT, CAP, FF), 1.0, 6.0, ((0, 32), (1, 32)))
    saved_up = normal_values(splits[4], (N_DP, EXPERTS, N_EXPERT, CAP, FF), 1.0, 6.0, ((0, 32), (1, 32)))
    w_down = normal_values(splits[5], (EXPERTS, FF, D), FF ** -0.5, 0.21875, ((0, 32),))
    return dict(grad_out=grad_out, probs=probs, routes=routes, saved_gate=saved_gate, saved_up=saved_up, w_down=w_down)


def silu_parts(gate_value):
    sigmoid = jax.nn.sigmoid(gate_value)
    return gate_value * sigmoid, sigmoid * (1.0 + gate_value * (1.0 - sigmoid))


def positions_of(route_block):
    flat_routes = route_block.reshape(-1).astype(jnp.int32)
    onehot = (flat_routes[:, None] == jnp.arange(EXPERTS, dtype=jnp.int32)[None, :]).astype(jnp.int32)
    before = jnp.cumsum(onehot, axis=0) - onehot
    slot_index = jnp.sum(before * onehot, axis=1).astype(jnp.int32)
    return (flat_routes * CAP + slot_index).astype(jnp.int32)


def dispatch(grad_block, prob_block, route_block):
    position = positions_of(route_block)
    repeated = jnp.repeat(grad_block, TOP, axis=0)
    sent_grad = jnp.zeros((EXPERTS * CAP, D), grad_block.dtype).at[position].set(repeated)
    sent_prob = jnp.zeros((EXPERTS * CAP,), prob_block.dtype).at[position].set(prob_block.reshape(-1))
    return sent_grad.reshape(EXPERTS, CAP, D), sent_prob.reshape(EXPERTS, CAP), position


def pick_slots(slot_values, positions):
    return jnp.take(slot_values, positions, axis=0)


def reference(grad_out, probs, routes, saved_gate, saved_up, w_down):
    grad_groups = grad_out.reshape(N_DP, N_EXPERT, TOK_DEV, D)
    prob_groups = probs.reshape(N_DP, N_EXPERT, TOK_DEV, TOP)
    route_groups = routes.reshape(N_DP, N_EXPERT, TOK_DEV, TOP)
    weight = w_down.astype(jnp.float32)

    def group_step(panel_sum, inputs):
        grad_rows, prob_rows, route_rows, gate_group, up_group = inputs
        sent_grad, sent_prob, position = jax.vmap(dispatch)(grad_rows, prob_rows, route_rows)
        sent_grad = jnp.swapaxes(sent_grad, 0, 1)
        sent_prob = jnp.swapaxes(sent_prob, 0, 1)
        gate_value = gate_group.astype(jnp.float32)
        up_value = up_group.astype(jnp.float32)
        activation, gate_slope = silu_parts(gate_value)
        hidden = (activation * up_value).astype(jnp.bfloat16)
        hidden_wide = hidden.astype(jnp.float32)
        grad_wide = sent_grad.astype(jnp.float32)
        expert_out = jnp.einsum("esck,ekd->escd", hidden_wide, weight)
        slot_grad = jnp.sum(grad_wide * expert_out, axis=-1)
        scaled = (sent_prob.astype(jnp.float32)[..., None] * grad_wide).astype(jnp.bfloat16)
        scaled_wide = scaled.astype(jnp.float32)
        grad_hidden = jnp.einsum("escd,ekd->esck", scaled_wide, weight)
        grad_up = (grad_hidden * activation).astype(jnp.bfloat16)
        grad_gate = (grad_hidden * up_value * gate_slope).astype(jnp.bfloat16)
        panel_sum = panel_sum + jnp.einsum("esck,escd->ekd", hidden_wide, scaled_wide)
        per_source = jnp.swapaxes(slot_grad, 0, 1).reshape(N_EXPERT, EXPERTS * CAP)
        route_grad = jax.vmap(pick_slots)(per_source, position)
        return panel_sum, (grad_gate, grad_up, route_grad.reshape(N_EXPERT, TOK_DEV, TOP))

    start_panel = jnp.zeros((EXPERTS, FF, D), jnp.float32)
    grad_weight, outputs = lax.scan(group_step, start_panel, (grad_groups, prob_groups, route_groups, saved_gate, saved_up))
    grad_gate, grad_up, route_grad = outputs
    return grad_gate, grad_up, grad_weight, route_grad.reshape(TOKENS, TOP)
```

```python
import functools

import jax
import jax.numpy as jnp
from jax import lax
from jax.experimental import pallas as pl
from jax.experimental.pallas import tpu as pltpu
from jax.sharding import PartitionSpec as P

MESH = pl.DeviceIdType.MESH
F32 = jnp.float32
BF16 = jnp.bfloat16
X_CHIPS = 4
CHUNK = 256
AHEAD = 3


def iota(shape, dim):
    return lax.broadcasted_iota(jnp.int32, shape, dim)


def nt_dot(a, b, **kw):
    return lax.dot_general(a, b, (((1,), (1,)), ((), ())), preferred_element_type=F32, **kw)


def kernel(
    nx, ny, nz, nk, cap,
    routes_ref, probs_ref, grad_hbm, gate_hbm, up_hbm, w_hbm,
    gg_hbm, gu_hbm, gw_ref, rg_ref,
    meta, gpair, sel, prow, parr, rows_ref, sent, arr, gate, up, wv,
    hid, act, slope, hpt, perm, u_ref, gwb, xr, ys, yr, sback, sarr, rgs, rgx,
    loc_sem, wsem, gsem, psend, precv, msem, zsend, zrecv, qsend, qrecv, xsend, xrecv, ysend, yrecv,
    ssend, srecv, rsem, osem,
):
    tok = gpair.shape[2]
    ff = gate.shape[1]
    blk = 2 * cap
    nrow = nz * blk
    dp, ex = lax.axis_index("dp"), lax.axis_index("expert")
    x, y = lax.rem(dp, nx), lax.div(dp, nx)
    z, c = lax.div(ex, 2), lax.rem(ex, 2)
    partner = {"expert": z * 2 + 1 - c}

    def z_peer(o):
        t = lax.rem(z + o, nz)
        return t, {"expert": t * 2 + c}

    def x_peer(o):
        t = lax.rem(x + o, nx)
        return t, {"dp": y * nx + t}

    def y_peer(o):
        t = lax.rem(y + o, ny)
        return t, {"dp": t * nx + x}

    def over(n, body):
        lax.fori_loop(1, n, lambda o, t: (body(o), t)[1], 0)

    def remote(src, dst, s, r, device):
        return pltpu.make_async_remote_copy(
            src_ref=src, dst_ref=dst, send_sem=s, recv_sem=r, device_id=device, device_id_type=MESH
        )

    bar = pltpu.get_barrier_semaphore()

    def greet(device):
        pl.semaphore_signal(bar, inc=1, device_id=device, device_id_type=MESH)

    over(nz, lambda o: greet(z_peer(o)[1]))
    over(ny, lambda o: greet(y_peer(o)[1]))
    over(nx, lambda o: greet(x_peer(o)[1]))
    greet(partner)

    gate_copy = pltpu.make_async_copy(gate_hbm, gate, loc_sem.at[0])
    up_copy = pltpu.make_async_copy(up_hbm, up, loc_sem.at[1])
    gate_copy.start()
    up_copy.start()

    def cols(k):
        return pl.ds(pl.multiple_of(k * CHUNK, CHUNK), CHUNK)

    def w_copy(k):
        return pltpu.make_async_copy(w_hbm.at[:, cols(k)], wv.at[k], wsem.at[k])

    def g_copy(k):
        return pltpu.make_async_copy(grad_hbm.at[:, cols(k)], gpair.at[k, c], gsem.at[k])

    def p_copy(k):
        return remote(grad_hbm.at[:, cols(k)], gpair.at[k, c], psend.at[k], precv.at[k], partner)

    def each_chunk(body):
        lax.fori_loop(0, nk, lambda k, t: (body(k), t)[1], 0)

    each_chunk(lambda k: g_copy(k).start())
    each_chunk(lambda k: w_copy(k).start())

    meta[c] = jnp.zeros(meta.shape[1:], F32)
    rgs[...] = jnp.zeros_like(rgs)
    meta[c, 0:2, :] = routes_ref[...].astype(F32)
    meta[c, 2:4, :] = probs_ref[...].astype(F32)

    gate_copy.wait()
    up_copy.wait()
    for j in range(0, ff, 128):
        gv = gate[:, j : j + 128].astype(F32)
        uv = up[:, j : j + 128].astype(F32)
        sg = 1.0 / (1.0 + jnp.exp(-gv))
        av = gv * sg
        hid[:, j : j + 128] = (av * uv).astype(BF16)
        act[:, j : j + 128] = av
        slope[:, j : j + 128] = uv * (sg * (1.0 + gv * (1.0 - sg)))
    q = iota((nrow, nrow), 0)
    r = iota((nrow, nrow), 1)
    source = lax.rem(q, 2 * nz)
    slot_of = lax.div(q, 2 * nz)
    perm[...] = (r == lax.div(source, 2) * blk + lax.rem(source, 2) * cap + slot_of).astype(F32).astype(BF16)
    u_ref[...] = jnp.zeros_like(u_ref)

    pl.semaphore_wait(bar, nz + ny + nx - 2)

    m_copy = remote(meta.at[c], meta.at[c], msem.at[0], msem.at[1], partner)
    m_copy.start()
    each_chunk(lambda k: p_copy(k).start())
    m_copy.wait_recv()

    experts = 2 * nz
    upper = (iota((tok, tok), 0) < iota((tok, tok), 1)).astype(F32).astype(BF16)
    parity = c.astype(F32)
    halves = ([], [])
    for s in range(2):
        named = [meta[s, k : k + 1, :] for k in range(2)]
        e = iota((experts, tok), 0).astype(F32)
        hot = [(e == n).astype(F32) for n in named]
        before = jnp.dot((hot[0] + hot[1]).astype(BF16), upper, preferred_element_type=F32)
        for k in range(2):
            slot = jnp.sum(hot[k] * before, axis=0, keepdims=True)
            chip = jnp.floor(named[k] * 0.5)
            mine = (named[k] - 2.0 * chip) == parity
            halves[k].append(jnp.where(mine, chip * blk + (s * cap) + slot, -1.0))
    row_iota = iota((nrow, 2 * tok), 0).astype(F32)
    chosen = None
    table = None
    for k in range(2):
        row = jnp.concatenate(halves[k], axis=1)
        rows_ref[k : k + 1, :] = row
        hit = row_iota == row
        chosen = hit if chosen is None else jnp.logical_or(chosen, hit)
        prob = jnp.concatenate([meta[s, 2 + k : 3 + k, :] for s in range(2)], axis=1)
        chip = jnp.floor((row + 0.5) * (1.0 / blk))
        lane = row - chip * blk
        by_chip = jnp.where(iota((nz, 2 * tok), 0).astype(F32) == chip, prob, 0.0).astype(BF16)
        by_lane = (iota((128, 2 * tok), 0).astype(F32) == lane).astype(F32).astype(BF16)
        part = nt_dot(by_chip, by_lane)
        table = part if table is None else table + part
    sel[...] = chosen.astype(F32).astype(BF16)
    prow[...] = table.reshape(nz, 1, 128)

    def z_copy(k, o):
        t, device = z_peer(o)
        return remote(sent.at[k, t], arr.at[k, z], zsend.at[k, o - 1], zrecv.at[k, o - 1], device)

    def q_copy(o):
        t, device = z_peer(o)
        return remote(prow.at[t], parr.at[z], qsend.at[o - 1], qrecv.at[o - 1], device)

    def s_copy(o):
        t, device = z_peer(o)
        return remote(sback.at[t], sarr.at[z], ssend.at[o - 1], srecv.at[o - 1], device)

    def x_copy(k, o):
        t, device = x_peer(o)
        return remote(gwb.at[k, :, t], xr.at[k, o - 1], xsend.at[k, o - 1], xrecv.at[k, o - 1], device)

    def y_copy(k, o):
        t, device = y_peer(o)
        return remote(ys.at[k, t], yr.at[k, o - 1], ysend.at[k, o - 1], yrecv.at[k, o - 1], device)

    def dispatch(k):
        g_copy(k).wait()
        p_copy(k).wait_recv()
        both = gpair[k].reshape(2 * tok, CHUNK)
        picked = jnp.dot(sel[...], both, preferred_element_type=F32).astype(BF16)
        sent[k] = picked.reshape(nz, blk, CHUNK)
        over(nz, lambda o: z_copy(k, o).start())
        arr[k, z] = sent[k, z]

    def combine(k):
        over(nz, lambda o: z_copy(k, o).wait_recv())
        got = arr[k].reshape(nrow, CHUNK)
        ordered = jnp.dot(perm[...], got, preferred_element_type=F32).astype(BF16)
        w_copy(k).wait()
        u_ref[...] += nt_dot(ordered, wv[k])
        panel = jnp.dot(hpt[...], ordered, preferred_element_type=F32).astype(BF16)
        gwb[k] = panel.reshape(gwb.shape[1:])
        over(nx, lambda o: x_copy(k, o).start())

    def x_sum(k):
        over(nx, lambda o: x_copy(k, o).wait_recv())
        total = gwb[k, :, x].astype(F32)
        for o in range(nx - 1):
            total = total + xr[k, o].astype(F32)
        ys[k] = total.astype(BF16)
        over(ny, lambda o: y_copy(k, o).start())

    def y_sum(k):
        over(ny, lambda o: y_copy(k, o).wait_recv())
        total = ys[k, y].astype(F32)
        for o in range(ny - 1):
            total = total + yr[k, o].astype(F32)
        gw_ref[:, cols(k)] = total

    over(nz, lambda o: q_copy(o).start())
    parr[z] = prow[z]
    lax.fori_loop(0, AHEAD, lambda k, t: (dispatch(k), t)[1], 0)

    over(nz, lambda o: q_copy(o).wait_recv())
    qz = lax.div(lax.rem(iota((nrow, nz), 0), 2 * nz), 2)
    pick_chip = (qz == iota((nrow, nz), 1)).astype(F32).astype(BF16)
    ql = iota((nrow, 128), 0)
    lane_of = lax.rem(ql, 2) * cap + lax.div(ql, 2 * nz)
    own_lane = (lane_of == iota((nrow, 128), 1)).astype(F32)
    spread = jnp.dot(pick_chip, parr[...].reshape(nz, 128).astype(BF16), preferred_element_type=F32)
    weight = jnp.sum(spread * own_lane, axis=1, keepdims=True)
    for j in range(0, ff, 128):
        hp = hid[:, j : j + 128].astype(F32) * weight
        hpt[j : j + 128, :] = hp.T.astype(BF16)
        act[:, j : j + 128] = act[:, j : j + 128] * weight
        slope[:, j : j + 128] = slope[:, j : j + 128] * weight

    def step(k, t):
        @pl.when(k + AHEAD < nk)
        def _():
            dispatch(k + AHEAD)

        combine(k)

        @pl.when(k >= 1)
        def _():
            x_sum(k - 1)

        @pl.when(k >= 2)
        def _():
            y_sum(k - 2)

        return t

    lax.fori_loop(0, nk, step, 0)

    sgrad = jnp.zeros((nrow, 1), F32)
    for j in range(0, ff, 128):
        sgrad = sgrad + jnp.sum(
            hid[:, j : j + 128].astype(F32) * u_ref[:, j : j + 128], axis=1, keepdims=True
        )
    to_chip = (
        lax.div(lax.rem(iota((nz, nrow), 1), 2 * nz), 2) == iota((nz, nrow), 0)
    ).astype(F32)
    back = jnp.dot(
        to_chip, own_lane * sgrad, preferred_element_type=F32, precision=lax.Precision.HIGHEST
    )
    sback[...] = back.reshape(nz, 1, 128)
    over(nz, lambda o: s_copy(o).start())
    sarr[z] = sback[z]

    x_sum(nk - 1)
    if nk >= 2:
        y_sum(nk - 2)

    for j in range(0, ff, 128):
        uv = u_ref[:, j : j + 128]
        gate[:, j : j + 128] = (uv * slope[:, j : j + 128]).astype(BF16)
        up[:, j : j + 128] = (uv * act[:, j : j + 128]).astype(BF16)
    gg_copy = pltpu.make_async_copy(gate, gg_hbm, osem.at[0])
    gu_copy = pltpu.make_async_copy(up, gu_hbm, osem.at[1])
    gg_copy.start()
    gu_copy.start()

    over(nz, lambda o: s_copy(o).wait_recv())
    returned = sarr[...].reshape(nz, 128)
    for k in range(2):
        row = rows_ref[k : k + 1, :]
        chip = jnp.floor((row + 0.5) * (1.0 / blk))
        lane = row - chip * blk
        by_lane = (iota((128, 2 * tok), 0).astype(F32) == lane).astype(F32)
        picked = jnp.dot(
            returned, by_lane, preferred_element_type=F32, precision=lax.Precision.HIGHEST
        )
        mine = iota((nz, 2 * tok), 0).astype(F32) == chip
        value = jnp.sum(jnp.where(mine, picked, 0.0), axis=0, keepdims=True)
        for s in range(2):
            rgs[s, k : k + 1, :] = value[:, s * tok : (s + 1) * tok]
    r_copy = remote(rgs.at[1 - c], rgx, rsem.at[0], rsem.at[1], partner)
    r_copy.start()
    y_sum(nk - 1)
    r_copy.wait_recv()
    rg_ref[...] = rgs[c][0:2, :] + rgx[0:2, :]

    gg_copy.wait()
    gu_copy.wait()
    m_copy.wait_send()
    r_copy.wait_send()
    over(nz, lambda o: q_copy(o).wait_send())
    over(nz, lambda o: s_copy(o).wait_send())

    def drain(k):
        p_copy(k).wait_send()
        over(nz, lambda o: z_copy(k, o).wait_send())
        over(nx, lambda o: x_copy(k, o).wait_send())
        over(ny, lambda o: y_copy(k, o).wait_send())

    each_chunk(drain)


def shards(nx, ny, nz, grad_out, probs, routes, saved_gate, saved_up, w_down):
    cap, ff = saved_gate.shape[3], saved_gate.shape[4]
    tok, width = grad_out.shape
    nk = width // CHUNK
    blk = 2 * cap
    nrow = nz * blk
    own = ff // (nx * ny)

    def flat(saved):
        return jnp.transpose(saved[0, 0], (1, 0, 2)).reshape(nrow, ff)

    vmem = pl.BlockSpec(memory_space=pltpu.VMEM)
    anywhere = pl.BlockSpec(memory_space=pl.ANY)
    dma = pltpu.SemaphoreType.DMA
    gg, gu, gw, rg = pl.pallas_call(
        functools.partial(kernel, nx, ny, nz, nk, cap),
        out_shape=(
            jax.ShapeDtypeStruct((nrow, ff), BF16),
            jax.ShapeDtypeStruct((nrow, ff), BF16),
            jax.ShapeDtypeStruct((own, width), F32),
            jax.ShapeDtypeStruct((2, tok), F32),
        ),
        in_specs=[vmem, vmem, anywhere, anywhere, anywhere, anywhere],
        out_specs=(anywhere, anywhere, vmem, vmem),
        scratch_shapes=[
            pltpu.VMEM((2, 8, tok), F32),
            pltpu.VMEM((nk, 2, tok, CHUNK), BF16),
            pltpu.VMEM((nrow, 2 * tok), BF16),
            pltpu.VMEM((nz, 1, 128), F32),
            pltpu.VMEM((nz, 1, 128), F32),
            pltpu.VMEM((8, 2 * tok), F32),
            pltpu.VMEM((nk, nz, blk, CHUNK), BF16),
            pltpu.VMEM((nk, nz, blk, CHUNK), BF16),
            pltpu.VMEM((nrow, ff), BF16),
            pltpu.VMEM((nrow, ff), BF16),
            pltpu.VMEM((nk, ff, CHUNK), BF16),
            pltpu.VMEM((nrow, ff), BF16),
            pltpu.VMEM((nrow, ff), F32),
            pltpu.VMEM((nrow, ff), F32),
            pltpu.VMEM((ff, nrow), BF16),
            pltpu.VMEM((nrow, nrow), BF16),
            pltpu.VMEM((nrow, ff), F32),
            pltpu.VMEM((nk, ny, nx, own, CHUNK), BF16),
            pltpu.VMEM((nk, nx - 1, ny, own, CHUNK), BF16),
            pltpu.VMEM((nk, ny, own, CHUNK), BF16),
            pltpu.VMEM((nk, ny - 1, own, CHUNK), BF16),
            pltpu.VMEM((nz, 1, 128), F32),
            pltpu.VMEM((nz, 1, 128), F32),
            pltpu.VMEM((2, 8, tok), F32),
            pltpu.VMEM((8, tok), F32),
            dma((2,)),
            dma((nk,)),
            dma((nk,)),
            dma((nk,)),
            dma((nk,)),
            dma((2,)),
            dma((nk, nz - 1)),
            dma((nk, nz - 1)),
            dma((nz - 1,)),
            dma((nz - 1,)),
            dma((nk, nx - 1)),
            dma((nk, nx - 1)),
            dma((nk, ny - 1)),
            dma((nk, ny - 1)),
            dma((nz - 1,)),
            dma((nz - 1,)),
            dma((2,)),
            dma((2,)),
        ],
        compiler_params=pltpu.CompilerParams(
            collective_id=0, has_side_effects=True, vmem_limit_bytes=56 * 1024 * 1024
        ),
        name="expert_backward",
    )(routes.T, probs.T, grad_out, flat(saved_gate), flat(saved_up), w_down[0])

    def unflat(value):
        return jnp.transpose(value.reshape(cap, 2 * nz, ff), (1, 0, 2))[None, None]

    return unflat(gg), unflat(gu), gw[None], rg.T


def solution(mesh):
    nx = X_CHIPS
    ny = mesh.shape["dp"] // nx
    nz = mesh.shape["expert"] // 2
    return jax.shard_map(
        functools.partial(shards, nx, ny, nz),
        mesh=mesh,
        in_specs=(
            P(("dp", "expert"), None),
            P(("dp", "expert"), None),
            P(("dp", "expert"), None),
            P("dp", "expert", None, None, None),
            P("dp", "expert", None, None, None),
            P("expert", None, None),
        ),
        out_specs=(
            P("dp", "expert", None, None, None),
            P("dp", "expert", None, None, None),
            P("expert", "dp", None),
            P(("dp", "expert"), None),
        ),
        check_vma=False,
    )
```

```python
import functools

import jax
import jax.numpy as jnp
from jax import lax
from jax.experimental import pallas as pl
from jax.experimental.pallas import tpu as pltpu
from jax.sharding import PartitionSpec as P

MESH = pl.DeviceIdType.MESH
F32 = jnp.float32
BF16 = jnp.bfloat16
X_CHIPS = 4
WIDTHS = (256, 512, 512, 384, 256, 128)
AHEAD = 3
VMEM_LIMIT = 44 * 1024 * 1024
WRITE_IN = pl.BlockSpec(memory_space=pl.ANY)


def iota(shape, dim):
    return lax.broadcasted_iota(jnp.int32, shape, dim)


def nt_dot(a, b, **kw):
    return lax.dot_general(a, b, (((1,), (1,)), ((), ())), preferred_element_type=F32, **kw)


def kernel(
    nx, ny, nz, cap, widths,
    routes_ref, probs_ref, grad_hbm, gate_hbm, up_hbm, w_hbm,
    gg_out, gu_out, gw_ref, rg_ref,
    meta, sel, prow, parr, rows_ref, gate, up, hid, act, slope, hpt, perm, u_ref,
    sback, sarr, rgs, rgx, gpair, sent, arr, wv, gwb, xr, ys, yr, loc_sem, pair_sem, chunk_sem, back_sem,
):
    nk = len(widths)
    starts = [sum(widths[:k]) for k in range(nk)]
    tok = rgx.shape[1]
    ff = gate.shape[1]
    blk = 2 * cap
    nrow = nz * blk
    dp, ex = lax.axis_index("dp"), lax.axis_index("expert")
    x, y = lax.rem(dp, nx), lax.div(dp, nx)
    z, c = lax.div(ex, 2), lax.rem(ex, 2)
    partner = {"expert": z * 2 + 1 - c}

    def z_peer(o):
        t = lax.rem(z + o, nz)
        return t, {"expert": t * 2 + c}

    def x_peer(o):
        t = lax.rem(x + o, nx)
        return t, {"dp": y * nx + t}

    def y_peer(o):
        t = lax.rem(y + o, ny)
        return t, {"dp": t * nx + x}

    def over(n, body):
        lax.fori_loop(1, n, lambda o, t: (body(o), t)[1], 0)

    def remote(src, dst, s, r, device):
        return pltpu.make_async_remote_copy(
            src_ref=src, dst_ref=dst, send_sem=s, recv_sem=r, device_id=device, device_id_type=MESH
        )

    bar = pltpu.get_barrier_semaphore()

    def greet(device):
        pl.semaphore_signal(bar, inc=1, device_id=device, device_id_type=MESH)

    over(nz, lambda o: greet(z_peer(o)[1]))
    over(ny, lambda o: greet(y_peer(o)[1]))
    over(nx, lambda o: greet(x_peer(o)[1]))
    greet(partner)

    def cols(k):
        return pl.ds(starts[k], widths[k])

    def w_copy(k):
        return pltpu.make_async_copy(w_hbm.at[:, cols(k)], wv[k], chunk_sem.at[k, 0])

    def g_copy(k):
        return pltpu.make_async_copy(grad_hbm.at[:, cols(k)], gpair[k].at[c], chunk_sem.at[k, 1])

    def p_copy(k):
        return remote(
            grad_hbm.at[:, cols(k)], gpair[k].at[c], chunk_sem.at[k, 2], chunk_sem.at[k, 3], partner
        )

    gate_copy = pltpu.make_async_copy(gate_hbm, gate, loc_sem.at[0])
    up_copy = pltpu.make_async_copy(up_hbm, up, loc_sem.at[1])
    g_copy(0).start()
    gate_copy.start()
    up_copy.start()
    for k in range(1, nk):
        g_copy(k).start()
    for k in range(nk):
        w_copy(k).start()

    meta[c] = jnp.zeros(meta.shape[1:], F32)
    rgs[...] = jnp.zeros_like(rgs)
    meta[c, 0:2, :] = routes_ref[...].astype(F32)
    meta[c, 2:4, :] = probs_ref[...].astype(F32)

    gate_copy.wait()
    up_copy.wait()
    for j in range(0, ff, 128):
        gv = gate[:, j : j + 128].astype(F32)
        uv = up[:, j : j + 128].astype(F32)
        sg = 1.0 / (1.0 + jnp.exp(-gv))
        av = gv * sg
        hid[:, j : j + 128] = (av * uv).astype(BF16)
        act[:, j : j + 128] = av
        slope[:, j : j + 128] = uv * (sg * (1.0 + gv * (1.0 - sg)))
    q = iota((nrow, nrow), 0)
    r = iota((nrow, nrow), 1)
    source = lax.rem(q, 2 * nz)
    slot_of = lax.div(q, 2 * nz)
    perm[...] = (r == lax.div(source, 2) * blk + lax.rem(source, 2) * cap + slot_of).astype(F32).astype(BF16)

    pl.semaphore_wait(bar, nz + ny + nx - 2)

    m_copy = remote(meta.at[c], meta.at[c], pair_sem.at[0], pair_sem.at[1], partner)
    m_copy.start()
    for k in range(nk):
        p_copy(k).start()
    m_copy.wait_recv()

    experts = 2 * nz
    upper = (iota((tok, tok), 0) < iota((tok, tok), 1)).astype(F32).astype(BF16)
    parity = c.astype(F32)
    halves = ([], [])
    for s in range(2):
        named = [meta[s, k : k + 1, :] for k in range(2)]
        e = iota((experts, tok), 0).astype(F32)
        hot = [(e == n).astype(F32) for n in named]
        before = jnp.dot((hot[0] + hot[1]).astype(BF16), upper, preferred_element_type=F32)
        for k in range(2):
            slot = jnp.sum(hot[k] * before, axis=0, keepdims=True)
            chip = jnp.floor(named[k] * 0.5)
            mine = (named[k] - 2.0 * chip) == parity
            halves[k].append(jnp.where(mine, chip * blk + (s * cap) + slot, -1.0))
    row_iota = iota((nrow, 2 * tok), 0).astype(F32)
    targets = [jnp.concatenate(halves[k], axis=1) for k in range(2)]
    chosen = jnp.logical_or(row_iota == targets[0], row_iota == targets[1])
    sel[...] = chosen.astype(F32).astype(BF16)
    for k in range(2):
        rows_ref[k : k + 1, :] = targets[k]

    def z_copy(k, o):
        t, device = z_peer(o)
        return remote(sent[k].at[t], arr[k].at[z], chunk_sem.at[k, 4], chunk_sem.at[k, 5], device)

    def z_all(k):
        part = arr[k].at[pl.ds(0, nz - 1)]
        return remote(part, part, chunk_sem.at[k, 4], chunk_sem.at[k, 5], partner)

    def x_copy(k, o):
        t, device = x_peer(o)
        return remote(gwb[k].at[:, t], xr[k].at[o - 1], chunk_sem.at[k, 6], chunk_sem.at[k, 7], device)

    def x_all(k):
        return remote(xr[k], xr[k], chunk_sem.at[k, 6], chunk_sem.at[k, 7], partner)

    def y_copy(k, o):
        t, device = y_peer(o)
        return remote(ys[k].at[t], yr[k].at[o - 1], chunk_sem.at[k, 8], chunk_sem.at[k, 9], device)

    def y_all(k):
        return remote(yr[k], yr[k], chunk_sem.at[k, 8], chunk_sem.at[k, 9], partner)

    def q_copy(o):
        t, device = z_peer(o)
        return remote(prow.at[t], parr.at[z], back_sem.at[0], back_sem.at[1], device)

    def s_copy(o):
        t, device = z_peer(o)
        return remote(sback.at[t], sarr.at[z], back_sem.at[2], back_sem.at[3], device)

    def q_all():
        part = parr.at[pl.ds(0, nz - 1)]
        return remote(part, part, back_sem.at[0], back_sem.at[1], partner)

    def s_all():
        part = sarr.at[pl.ds(0, nz - 1)]
        return remote(part, part, back_sem.at[2], back_sem.at[3], partner)

    def dispatch(k):
        g_copy(k).wait()
        p_copy(k).wait_recv()
        both = gpair[k][...].reshape(2 * tok, widths[k])
        picked = jnp.dot(sel[...], both, preferred_element_type=F32).astype(BF16)
        sent[k][...] = picked.reshape(nz, blk, widths[k])
        over(nz, lambda o: z_copy(k, o).start())
        arr[k][z] = sent[k][z]

    def combine(k):
        z_all(k).wait_recv()
        got = arr[k][...].reshape(nrow, widths[k])
        ordered = jnp.dot(perm[...], got, preferred_element_type=F32).astype(BF16)
        w_copy(k).wait()
        panel = jnp.dot(hpt[...], ordered, preferred_element_type=F32).astype(BF16)
        gwb[k][...] = panel.reshape(gwb[k].shape)
        over(nx, lambda o: x_copy(k, o).start())
        part = nt_dot(ordered, wv[k][...])
        if k == 0:
            u_ref[...] = part
        else:
            u_ref[...] += part

    def x_sum(k):
        x_all(k).wait_recv()
        total = gwb[k][:, x].astype(F32)
        for o in range(nx - 1):
            total = total + xr[k][o].astype(F32)
        ys[k][...] = total.astype(BF16)
        over(ny, lambda o: y_copy(k, o).start())

    def y_sum(k):
        y_all(k).wait_recv()
        total = ys[k][y].astype(F32)
        for o in range(ny - 1):
            total = total + yr[k][o].astype(F32)
        gw_ref[:, cols(k)] = total

    dispatch(0)

    table = None
    for k in range(2):
        prob = jnp.concatenate([meta[s, 2 + k : 3 + k, :] for s in range(2)], axis=1)
        chip = jnp.floor((targets[k] + 0.5) * (1.0 / blk))
        lane = targets[k] - chip * blk
        by_chip = jnp.where(iota((nz, 2 * tok), 0).astype(F32) == chip, prob, 0.0).astype(BF16)
        by_lane = (iota((128, 2 * tok), 0).astype(F32) == lane).astype(F32).astype(BF16)
        part = nt_dot(by_chip, by_lane)
        table = part if table is None else table + part
    prow[...] = table.reshape(nz, 1, 128)
    over(nz, lambda o: q_copy(o).start())
    parr[z] = prow[z]
    for k in range(1, AHEAD):
        dispatch(k)

    q_all().wait_recv()
    qz = lax.div(lax.rem(iota((nrow, nz), 0), 2 * nz), 2)
    pick_chip = (qz == iota((nrow, nz), 1)).astype(F32).astype(BF16)
    ql = iota((nrow, 128), 0)
    lane_of = lax.rem(ql, 2) * cap + lax.div(ql, 2 * nz)
    own_lane = (lane_of == iota((nrow, 128), 1)).astype(F32)
    spread = jnp.dot(pick_chip, parr[...].reshape(nz, 128).astype(BF16), preferred_element_type=F32)
    weight = jnp.sum(spread * own_lane, axis=1, keepdims=True)
    for j in range(0, ff, 128):
        hp = hid[:, j : j + 128].astype(F32) * weight
        hpt[j : j + 128, :] = hp.T.astype(BF16)
        act[:, j : j + 128] = act[:, j : j + 128] * weight
        slope[:, j : j + 128] = slope[:, j : j + 128] * weight

    for k in range(nk):
        if k + AHEAD < nk:
            dispatch(k + AHEAD)
        combine(k)
        if k >= 1 and k < nk - 1:
            x_sum(k - 1)
        if k >= 2 and k < nk - 1:
            y_sum(k - 2)

    sgrad = jnp.zeros((nrow, 1), F32)
    for j in range(0, ff, 128):
        sgrad = sgrad + jnp.sum(
            hid[:, j : j + 128].astype(F32) * u_ref[:, j : j + 128], axis=1, keepdims=True
        )
    to_chip = (
        lax.div(lax.rem(iota((nz, nrow), 1), 2 * nz), 2) == iota((nz, nrow), 0)
    ).astype(F32)
    back = jnp.dot(
        to_chip, own_lane * sgrad, preferred_element_type=F32, precision=lax.Precision.HIGHEST
    )
    sback[...] = back.reshape(nz, 1, 128)
    over(nz, lambda o: s_copy(o).start())
    sarr[z] = sback[z]

    if nk >= 2:
        x_sum(nk - 2)
    if nk >= 3:
        y_sum(nk - 3)
    x_sum(nk - 1)

    for j in range(0, ff, 128):
        uv = u_ref[:, j : j + 128]
        gg_out[:, j : j + 128] = (uv * slope[:, j : j + 128]).astype(BF16)
        gu_out[:, j : j + 128] = (uv * act[:, j : j + 128]).astype(BF16)
    if nk >= 2:
        y_sum(nk - 2)

    masks = []
    for k in range(2):
        row = rows_ref[k : k + 1, :]
        chip = jnp.floor((row + 0.5) * (1.0 / blk))
        lane = row - chip * blk
        masks.append(
            (
                (iota((128, 2 * tok), 0).astype(F32) == lane).astype(F32),
                iota((nz, 2 * tok), 0).astype(F32) == chip,
            )
        )
    s_all().wait_recv()
    returned = sarr[...].reshape(nz, 128)
    for k in range(2):
        by_lane, mine = masks[k]
        picked = jnp.dot(
            returned, by_lane, preferred_element_type=F32, precision=lax.Precision.HIGHEST
        )
        value = jnp.sum(jnp.where(mine, picked, 0.0), axis=0, keepdims=True)
        for s in range(2):
            rgs[s, k : k + 1, :] = value[:, s * tok : (s + 1) * tok]
    r_copy = remote(rgs.at[1 - c], rgx, pair_sem.at[2], pair_sem.at[3], partner)
    r_copy.start()

    m_copy.wait_send()
    q_all().wait_send()
    s_all().wait_send()
    for k in range(nk):
        p_copy(k).wait_send()
        z_all(k).wait_send()
        x_all(k).wait_send()
    for k in range(nk - 1):
        y_all(k).wait_send()
    r_copy.wait_recv()
    rg_ref[...] = rgs[c][0:2, :] + rgx[0:2, :]
    r_copy.wait_send()
    y_sum(nk - 1)
    y_all(nk - 1).wait_send()


def write_out(n, *refs):
    ins, outs, sem = refs[:n], refs[n : 2 * n], refs[2 * n]
    copies = [pltpu.make_async_copy(ins[i], outs[i], sem.at[i]) for i in range(n)]
    for copy in copies:
        copy.start()
    for copy in copies:
        copy.wait()


def shards(nx, ny, nz, grad_out, probs, routes, saved_gate, saved_up, w_down):
    cap, ff = saved_gate.shape[3], saved_gate.shape[4]
    tok, width = grad_out.shape
    widths = WIDTHS
    blk = 2 * cap
    nrow = nz * blk
    own = ff // (nx * ny)

    def flat(saved):
        return jnp.transpose(saved[0, 0], (1, 0, 2)).reshape(nrow, ff)

    vmem = pl.BlockSpec(memory_space=pltpu.VMEM)
    anywhere = pl.BlockSpec(memory_space=pl.ANY)
    in_hbm = pl.BlockSpec(memory_space=pltpu.HBM)
    dma = pltpu.SemaphoreType.DMA

    def per_chunk(*shape):
        return tuple(pltpu.VMEM(shape + (wide,), BF16) for wide in widths)

    shapes = (
        jax.ShapeDtypeStruct((nrow, ff), BF16),
        jax.ShapeDtypeStruct((nrow, ff), BF16),
        jax.ShapeDtypeStruct((own, width), F32),
        jax.ShapeDtypeStruct((2, tok), F32),
    )
    results = pl.pallas_call(
        functools.partial(kernel, nx, ny, nz, cap, widths),
        out_shape=shapes,
        in_specs=[vmem, vmem, in_hbm, in_hbm, in_hbm, in_hbm],
        out_specs=(vmem, vmem, vmem, vmem),
        scratch_shapes=[
            pltpu.VMEM((2, 8, tok), F32),
            pltpu.VMEM((nrow, 2 * tok), BF16),
            pltpu.VMEM((nz, 1, 128), F32),
            pltpu.VMEM((nz, 1, 128), F32),
            pltpu.VMEM((8, 2 * tok), F32),
            pltpu.VMEM((nrow, ff), BF16),
            pltpu.VMEM((nrow, ff), BF16),
            pltpu.VMEM((nrow, ff), BF16),
            pltpu.VMEM((nrow, ff), F32),
            pltpu.VMEM((nrow, ff), F32),
            pltpu.VMEM((ff, nrow), BF16),
            pltpu.VMEM((nrow, nrow), BF16),
            pltpu.VMEM((nrow, ff), F32),
            pltpu.VMEM((nz, 1, 128), F32),
            pltpu.VMEM((nz, 1, 128), F32),
            pltpu.VMEM((2, 8, tok), F32),
            pltpu.VMEM((8, tok), F32),
            per_chunk(2, tok),
            per_chunk(nz, blk),
            per_chunk(nz, blk),
            per_chunk(ff),
            per_chunk(ny, nx, own),
            per_chunk(nx - 1, ny, own),
            per_chunk(ny, own),
            per_chunk(ny - 1, own),
            dma((2,)),
            dma((4,)),
            dma((len(widths), 10)),
            dma((4,)),
        ],
        compiler_params=pltpu.CompilerParams(
            collective_id=0, has_side_effects=True, vmem_limit_bytes=VMEM_LIMIT
        ),
        name="expert_backward",
    )(*[
        pltpu.with_memory_space_constraint(value, pltpu.HBM)
        for value in (routes.T, probs.T, grad_out, flat(saved_gate), flat(saved_up), w_down[0])
    ])
    gg, gu, gw, rg = pl.pallas_call(
        functools.partial(write_out, len(shapes)),
        out_shape=shapes,
        in_specs=[WRITE_IN] * len(shapes),
        out_specs=(anywhere,) * len(shapes),
        scratch_shapes=[dma((len(shapes),))],
        compiler_params=pltpu.CompilerParams(vmem_limit_bytes=4 * 1024 * 1024),
        name="write_out",
    )(*results)

    def unflat(value):
        return jnp.transpose(value.reshape(cap, 2 * nz, ff), (1, 0, 2))[None, None]

    return unflat(gg), unflat(gu), gw[None], rg.T


def solution(mesh):
    nx = X_CHIPS
    ny = mesh.shape["dp"] // nx
    nz = mesh.shape["expert"] // 2
    return jax.shard_map(
        functools.partial(shards, nx, ny, nz),
        mesh=mesh,
        in_specs=(
            P(("dp", "expert"), None),
            P(("dp", "expert"), None),
            P(("dp", "expert"), None),
            P("dp", "expert", None, None, None),
            P("dp", "expert", None, None, None),
            P("expert", None, None),
        ),
        out_specs=(
            P("dp", "expert", None, None, None),
            P("dp", "expert", None, None, None),
            P("expert", "dp", None),
            P(("dp", "expert"), None),
        ),
        check_vma=False,
    )
```

```python
import functools

import jax
import jax.numpy as jnp
from jax import lax
from jax.experimental import pallas as pl
from jax.experimental.pallas import tpu as pltpu
from jax.sharding import PartitionSpec as P

MESH = pl.DeviceIdType.MESH
F32 = jnp.float32
BF16 = jnp.bfloat16
X_CHIPS = 4
WIDTHS = (256, 512, 512, 384, 256, 128)
AHEAD = 3
VMEM_LIMIT = 44 * 1024 * 1024
WRITE_IN = pl.BlockSpec(memory_space=pl.ANY)


def iota(shape, dim):
    return lax.broadcasted_iota(jnp.int32, shape, dim)


def nt_dot(a, b, **kw):
    return lax.dot_general(a, b, (((1,), (1,)), ((), ())), preferred_element_type=F32, **kw)


def kernel(
    nx, ny, nz, cap, widths,
    routes_hbm, probs_hbm, grad_hbm, gate_hbm, up_hbm, w_hbm,
    gg_out, gu_out, gw_ref, rg_ref,
    routes_ref, probs_ref, meta, sel, prow, parr, rows_ref, gate, up, hid, act, slope, hpt, perm, u_ref,
    sback, sarr, rgs, rgx, gpair, sent, arr, wv, gwb, xr, ys, yr, loc_sem, pair_sem, chunk_sem, back_sem,
):
    nk = len(widths)
    starts = [sum(widths[:k]) for k in range(nk)]
    tok = rgx.shape[1]
    ff = gate.shape[1]
    blk = 2 * cap
    nrow = nz * blk
    dp, ex = lax.axis_index("dp"), lax.axis_index("expert")
    x, y = lax.rem(dp, nx), lax.div(dp, nx)
    z, c = lax.div(ex, 2), lax.rem(ex, 2)
    partner = {"expert": z * 2 + 1 - c}

    def z_peer(o):
        t = lax.rem(z + o, nz)
        return t, {"expert": t * 2 + c}

    def x_peer(o):
        t = lax.rem(x + o, nx)
        return t, {"dp": y * nx + t}

    def y_peer(o):
        t = lax.rem(y + o, ny)
        return t, {"dp": t * nx + x}

    def over(n, body):
        lax.fori_loop(1, n, lambda o, t: (body(o), t)[1], 0)

    def far_first(n, body):
        def one(i, t):
            body(n // 2 + (1 - 2 * lax.rem(i, 2)) * lax.div(i + 1, 2))
            return t

        lax.fori_loop(0, n - 1, one, 0)

    def remote(src, dst, s, r, device):
        return pltpu.make_async_remote_copy(
            src_ref=src, dst_ref=dst, send_sem=s, recv_sem=r, device_id=device, device_id_type=MESH
        )

    bar = pltpu.get_barrier_semaphore()

    def greet(device):
        pl.semaphore_signal(bar, inc=1, device_id=device, device_id_type=MESH)

    far_first(nz, lambda o: greet(z_peer(o)[1]))
    over(ny, lambda o: greet(y_peer(o)[1]))
    over(nx, lambda o: greet(x_peer(o)[1]))
    greet(partner)

    def cols(k):
        return pl.ds(starts[k], widths[k])

    def w_copy(k):
        return pltpu.make_async_copy(w_hbm.at[:, cols(k)], wv[k], chunk_sem.at[k, 0])

    def g_copy(k):
        return pltpu.make_async_copy(grad_hbm.at[:, cols(k)], gpair[k].at[c], chunk_sem.at[k, 1])

    def p_copy(k):
        return remote(
            grad_hbm.at[:, cols(k)], gpair[k].at[c], chunk_sem.at[k, 2], chunk_sem.at[k, 3], partner
        )

    gate_copy = pltpu.make_async_copy(gate_hbm, gate, loc_sem.at[0])
    up_copy = pltpu.make_async_copy(up_hbm, up, loc_sem.at[1])
    routes_copy = pltpu.make_async_copy(routes_hbm, routes_ref, loc_sem.at[2])
    probs_copy = pltpu.make_async_copy(probs_hbm, probs_ref, loc_sem.at[3])
    routes_copy.start()
    probs_copy.start()
    g_copy(0).start()
    gate_copy.start()
    up_copy.start()
    for k in range(1, nk):
        g_copy(k).start()
    for k in range(nk):
        w_copy(k).start()

    rgs[...] = jnp.zeros_like(rgs)
    routes_copy.wait()
    probs_copy.wait()
    named = routes_ref[...].astype(F32)
    experts = 2 * nz
    upper = (iota((tok, tok), 0) < iota((tok, tok), 1)).astype(F32).astype(BF16)
    e = iota((experts, tok), 0).astype(F32)
    hot = [(e == named[k : k + 1, :]).astype(F32) for k in range(2)]
    before = jnp.dot((hot[0] + hot[1]).astype(BF16), upper, preferred_element_type=F32)
    chip = jnp.floor(named * 0.5)
    meta[c, 0:2, :] = chip * blk
    meta[c, 2:4, :] = named - 2.0 * chip
    for k in range(2):
        meta[c, 4 + k : 5 + k, :] = jnp.sum(hot[k] * before, axis=0, keepdims=True) + (c * cap).astype(F32)
    meta[c, 6:8, :] = probs_ref[...].astype(F32)

    gate_copy.wait()
    up_copy.wait()
    for j in range(0, ff, 128):
        gv = gate[:, j : j + 128].astype(F32)
        uv = up[:, j : j + 128].astype(F32)
        sg = 1.0 / (1.0 + jnp.exp(-gv))
        av = gv * sg
        hid[:, j : j + 128] = (av * uv).astype(BF16)
        act[:, j : j + 128] = av
        slope[:, j : j + 128] = uv * (sg * (1.0 + gv * (1.0 - sg)))
    q = iota((nrow, nrow), 0)
    r = iota((nrow, nrow), 1)
    source = lax.rem(q, 2 * nz)
    slot_of = lax.div(q, 2 * nz)
    perm[...] = (r == lax.div(source, 2) * blk + lax.rem(source, 2) * cap + slot_of).astype(F32).astype(BF16)

    pl.semaphore_wait(bar, nz + ny + nx - 2)

    m_copy = remote(meta.at[c], meta.at[c], pair_sem.at[0], pair_sem.at[1], partner)
    m_copy.start()
    for k in range(nk):
        p_copy(k).start()
    m_copy.wait_recv()

    parity = c.astype(F32)
    both_halves = jnp.concatenate([meta[0], meta[1]], axis=1)
    target = jnp.where(both_halves[2:4] == parity, both_halves[0:2] + both_halves[4:6], -1.0)
    row_iota = iota((nrow, 2 * tok), 0).astype(F32)
    targets = [target[k : k + 1] for k in range(2)]
    chosen = jnp.logical_or(row_iota == targets[0], row_iota == targets[1])
    sel[...] = chosen.astype(F32).astype(BF16)
    for k in range(2):
        rows_ref[k : k + 1, :] = targets[k]

    def z_copy(k, o):
        t, device = z_peer(o)
        return remote(sent[k].at[t], arr[k].at[z], chunk_sem.at[k, 4], chunk_sem.at[k, 5], device)

    def z_all(k):
        part = arr[k].at[pl.ds(0, nz - 1)]
        return remote(part, part, chunk_sem.at[k, 4], chunk_sem.at[k, 5], partner)

    def x_copy(k, o):
        t, device = x_peer(o)
        return remote(gwb[k].at[:, t], xr[k].at[o - 1], chunk_sem.at[k, 6], chunk_sem.at[k, 7], device)

    def x_all(k):
        return remote(xr[k], xr[k], chunk_sem.at[k, 6], chunk_sem.at[k, 7], partner)

    def y_copy(k, o):
        t, device = y_peer(o)
        return remote(ys[k].at[t], yr[k].at[o - 1], chunk_sem.at[k, 8], chunk_sem.at[k, 9], device)

    def y_all(k):
        return remote(yr[k], yr[k], chunk_sem.at[k, 8], chunk_sem.at[k, 9], partner)

    def q_copy(o):
        t, device = z_peer(o)
        return remote(prow.at[t], parr.at[z], back_sem.at[0], back_sem.at[1], device)

    def s_copy(o):
        t, device = z_peer(o)
        return remote(sback.at[t], sarr.at[z], back_sem.at[2], back_sem.at[3], device)

    def q_all():
        part = parr.at[pl.ds(0, nz - 1)]
        return remote(part, part, back_sem.at[0], back_sem.at[1], partner)

    def s_all():
        part = sarr.at[pl.ds(0, nz - 1)]
        return remote(part, part, back_sem.at[2], back_sem.at[3], partner)

    def dispatch(k):
        g_copy(k).wait()
        p_copy(k).wait_recv()
        both = gpair[k][...].reshape(2 * tok, widths[k])
        picked = jnp.dot(sel[...], both, preferred_element_type=F32).astype(BF16)
        sent[k][...] = picked.reshape(nz, blk, widths[k])
        far_first(nz, lambda o: z_copy(k, o).start())
        arr[k][z] = sent[k][z]

    def combine(k):
        z_all(k).wait_recv()
        got = arr[k][...].reshape(nrow, widths[k])
        ordered = jnp.dot(perm[...], got, preferred_element_type=F32).astype(BF16)
        w_copy(k).wait()
        panel = jnp.dot(hpt[...], ordered, preferred_element_type=F32).astype(BF16)
        gwb[k][...] = panel.reshape(gwb[k].shape)
        far_first(nx, lambda o: x_copy(k, o).start())
        part = nt_dot(ordered, wv[k][...])
        if k == 0:
            u_ref[...] = part
        else:
            u_ref[...] += part

    def x_sum(k):
        x_all(k).wait_recv()
        total = gwb[k][:, x].astype(F32)
        for o in range(nx - 1):
            total = total + xr[k][o].astype(F32)
        ys[k][...] = total.astype(BF16)
        far_first(ny, lambda o: y_copy(k, o).start())

    def y_sum(k):
        y_all(k).wait_recv()
        total = ys[k][y].astype(F32)
        for o in range(ny - 1):
            total = total + yr[k][o].astype(F32)
        gw_ref[:, cols(k)] = total

    dispatch(0)

    table = None
    for k in range(2):
        prob = both_halves[6 + k : 7 + k]
        chip = jnp.floor((targets[k] + 0.5) * (1.0 / blk))
        lane = targets[k] - chip * blk
        by_chip = jnp.where(iota((nz, 2 * tok), 0).astype(F32) == chip, prob, 0.0).astype(BF16)
        by_lane = (iota((128, 2 * tok), 0).astype(F32) == lane).astype(F32).astype(BF16)
        part = nt_dot(by_chip, by_lane)
        table = part if table is None else table + part
    prow[...] = table.reshape(nz, 1, 128)
    far_first(nz, lambda o: q_copy(o).start())
    parr[z] = prow[z]
    for k in range(1, AHEAD):
        dispatch(k)

    q_all().wait_recv()
    qz = lax.div(lax.rem(iota((nrow, nz), 0), 2 * nz), 2)
    pick_chip = (qz == iota((nrow, nz), 1)).astype(F32).astype(BF16)
    ql = iota((nrow, 128), 0)
    lane_of = lax.rem(ql, 2) * cap + lax.div(ql, 2 * nz)
    own_lane = (lane_of == iota((nrow, 128), 1)).astype(F32)
    spread = jnp.dot(pick_chip, parr[...].reshape(nz, 128).astype(BF16), preferred_element_type=F32)
    weight = jnp.sum(spread * own_lane, axis=1, keepdims=True)
    for j in range(0, ff, 128):
        hp = hid[:, j : j + 128].astype(F32) * weight
        hpt[j : j + 128, :] = hp.T.astype(BF16)
        act[:, j : j + 128] = act[:, j : j + 128] * weight
        slope[:, j : j + 128] = slope[:, j : j + 128] * weight

    for k in range(nk):
        if k + AHEAD < nk:
            dispatch(k + AHEAD)
        combine(k)
        if k >= 1 and k < nk - 1:
            x_sum(k - 1)
        if k >= 2 and k < nk - 1:
            y_sum(k - 2)

    sgrad = jnp.zeros((nrow, 1), F32)
    for j in range(0, ff, 128):
        sgrad = sgrad + jnp.sum(
            hid[:, j : j + 128].astype(F32) * u_ref[:, j : j + 128], axis=1, keepdims=True
        )
    to_chip = (
        lax.div(lax.rem(iota((nz, nrow), 1), 2 * nz), 2) == iota((nz, nrow), 0)
    ).astype(F32)
    back = jnp.dot(
        to_chip, own_lane * sgrad, preferred_element_type=F32, precision=lax.Precision.HIGHEST
    )
    sback[...] = back.reshape(nz, 1, 128)
    far_first(nz, lambda o: s_copy(o).start())
    sarr[z] = sback[z]

    if nk >= 2:
        x_sum(nk - 2)
    if nk >= 3:
        y_sum(nk - 3)
    x_sum(nk - 1)

    for j in range(0, ff, 128):
        uv = u_ref[:, j : j + 128]
        gg_out[:, j : j + 128] = (uv * slope[:, j : j + 128]).astype(BF16)
        gu_out[:, j : j + 128] = (uv * act[:, j : j + 128]).astype(BF16)
    if nk >= 2:
        y_sum(nk - 2)

    masks = []
    for k in range(2):
        row = rows_ref[k : k + 1, :]
        chip = jnp.floor((row + 0.5) * (1.0 / blk))
        lane = row - chip * blk
        masks.append(
            (
                (iota((128, 2 * tok), 0).astype(F32) == lane).astype(F32),
                iota((nz, 2 * tok), 0).astype(F32) == chip,
            )
        )
    s_all().wait_recv()
    returned = sarr[...].reshape(nz, 128)
    for k in range(2):
        by_lane, mine = masks[k]
        picked = jnp.dot(
            returned, by_lane, preferred_element_type=F32, precision=lax.Precision.HIGHEST
        )
        value = jnp.sum(jnp.where(mine, picked, 0.0), axis=0, keepdims=True)
        for s in range(2):
            rgs[s, k : k + 1, :] = value[:, s * tok : (s + 1) * tok]
    r_copy = remote(rgs.at[1 - c], rgx, pair_sem.at[2], pair_sem.at[3], partner)
    r_copy.start()

    m_copy.wait_send()
    q_all().wait_send()
    s_all().wait_send()
    for k in range(nk):
        p_copy(k).wait_send()
        z_all(k).wait_send()
        x_all(k).wait_send()
    for k in range(nk - 1):
        y_all(k).wait_send()
    r_copy.wait_recv()
    rg_ref[...] = rgs[c][0:2, :] + rgx[0:2, :]
    r_copy.wait_send()
    y_sum(nk - 1)
    y_all(nk - 1).wait_send()


def write_out(n, *refs):
    ins, outs, sem = refs[:n], refs[n : 2 * n], refs[2 * n]
    copies = [pltpu.make_async_copy(ins[i], outs[i], sem.at[i]) for i in range(n)]
    for copy in copies:
        copy.start()
    for copy in copies:
        copy.wait()


def shards(nx, ny, nz, grad_out, probs, routes, saved_gate, saved_up, w_down):
    cap, ff = saved_gate.shape[3], saved_gate.shape[4]
    tok, width = grad_out.shape
    widths = WIDTHS
    blk = 2 * cap
    nrow = nz * blk
    own = ff // (nx * ny)

    def flat(saved):
        return jnp.transpose(saved[0, 0], (1, 0, 2)).reshape(nrow, ff)

    vmem = pl.BlockSpec(memory_space=pltpu.VMEM)
    anywhere = pl.BlockSpec(memory_space=pl.ANY)
    in_hbm = pl.BlockSpec(memory_space=pltpu.HBM)
    dma = pltpu.SemaphoreType.DMA

    def per_chunk(*shape):
        return tuple(pltpu.VMEM(shape + (wide,), BF16) for wide in widths)

    shapes = (
        jax.ShapeDtypeStruct((nrow, ff), BF16),
        jax.ShapeDtypeStruct((nrow, ff), BF16),
        jax.ShapeDtypeStruct((own, width), F32),
        jax.ShapeDtypeStruct((2, tok), F32),
    )
    results = pl.pallas_call(
        functools.partial(kernel, nx, ny, nz, cap, widths),
        out_shape=shapes,
        in_specs=[in_hbm] * 6,
        out_specs=(vmem, vmem, vmem, vmem),
        scratch_shapes=[
            pltpu.VMEM((2, tok), jnp.int32),
            pltpu.VMEM((2, tok), BF16),
            pltpu.VMEM((2, 8, tok), F32),
            pltpu.VMEM((nrow, 2 * tok), BF16),
            pltpu.VMEM((nz, 1, 128), F32),
            pltpu.VMEM((nz, 1, 128), F32),
            pltpu.VMEM((8, 2 * tok), F32),
            pltpu.VMEM((nrow, ff), BF16),
            pltpu.VMEM((nrow, ff), BF16),
            pltpu.VMEM((nrow, ff), BF16),
            pltpu.VMEM((nrow, ff), F32),
            pltpu.VMEM((nrow, ff), F32),
            pltpu.VMEM((ff, nrow), BF16),
            pltpu.VMEM((nrow, nrow), BF16),
            pltpu.VMEM((nrow, ff), F32),
            pltpu.VMEM((nz, 1, 128), F32),
            pltpu.VMEM((nz, 1, 128), F32),
            pltpu.VMEM((2, 8, tok), F32),
            pltpu.VMEM((8, tok), F32),
            per_chunk(2, tok),
            per_chunk(nz, blk),
            per_chunk(nz, blk),
            per_chunk(ff),
            per_chunk(ny, nx, own),
            per_chunk(nx - 1, ny, own),
            per_chunk(ny, own),
            per_chunk(ny - 1, own),
            dma((4,)),
            dma((4,)),
            dma((len(widths), 10)),
            dma((4,)),
        ],
        compiler_params=pltpu.CompilerParams(
            collective_id=0, has_side_effects=True, vmem_limit_bytes=VMEM_LIMIT
        ),
        name="expert_backward",
    )(*[
        pltpu.with_memory_space_constraint(value, pltpu.HBM)
        for value in (routes.T, probs.T, grad_out, flat(saved_gate), flat(saved_up), w_down[0])
    ])
    gg, gu, gw, rg = pl.pallas_call(
        functools.partial(write_out, len(shapes)),
        out_shape=shapes,
        in_specs=[WRITE_IN] * len(shapes),
        out_specs=(anywhere,) * len(shapes),
        scratch_shapes=[dma((len(shapes),))],
        compiler_params=pltpu.CompilerParams(vmem_limit_bytes=4 * 1024 * 1024),
        name="write_out",
    )(*results)

    def unflat(value):
        return jnp.transpose(value.reshape(cap, 2 * nz, ff), (1, 0, 2))[None, None]

    return unflat(gg), unflat(gu), gw[None], rg.T


def solution(mesh):
    nx = X_CHIPS
    ny = mesh.shape["dp"] // nx
    nz = mesh.shape["expert"] // 2
    return jax.shard_map(
        functools.partial(shards, nx, ny, nz),
        mesh=mesh,
        in_specs=(
            P(("dp", "expert"), None),
            P(("dp", "expert"), None),
            P(("dp", "expert"), None),
            P("dp", "expert", None, None, None),
            P("dp", "expert", None, None, None),
            P("expert", None, None),
        ),
        out_specs=(
            P("dp", "expert", None, None, None),
            P("dp", "expert", None, None, None),
            P("expert", "dp", None),
            P(("dp", "expert"), None),
        ),
        check_vma=False,
    )
```

```python
import functools

import jax
import jax.numpy as jnp
from jax import lax
from jax.experimental import pallas as pl
from jax.experimental.pallas import tpu as pltpu
from jax.sharding import PartitionSpec as P

MESH = pl.DeviceIdType.MESH
F32 = jnp.float32
BF16 = jnp.bfloat16
X_CHIPS = 4
WIDTHS = (128, 384, 512, 512, 256, 128, 128)
AHEAD = 3
VMEM_LIMIT = 44 * 1024 * 1024
WRITE_IN = pl.BlockSpec(memory_space=pl.ANY)


def iota(shape, dim):
    return lax.broadcasted_iota(jnp.int32, shape, dim)


def nt_dot(a, b, **kw):
    return lax.dot_general(a, b, (((1,), (1,)), ((), ())), preferred_element_type=F32, **kw)


def kernel(
    nx, ny, nz, cap, widths,
    routes_hbm, probs_hbm, grad_hbm, gate_hbm, up_hbm, w_hbm,
    gg_out, gu_out, gw_ref, rg_ref,
    routes_ref, probs_ref, meta, sel, prow, parr, rows_ref, gate, up, hid, act, slope, hpt, perm, u_ref,
    sback, sarr, rgs, rgx, gpair, sent, arr, wv, gwb, xr, ys, yr, loc_sem, pair_sem, chunk_sem, back_sem,
):
    nk = len(widths)
    starts = [sum(widths[:k]) for k in range(nk)]
    tok = rgx.shape[1]
    ff = gate.shape[1]
    blk = 2 * cap
    nrow = nz * blk
    dp, ex = lax.axis_index("dp"), lax.axis_index("expert")
    x, y = lax.rem(dp, nx), lax.div(dp, nx)
    z, c = lax.div(ex, 2), lax.rem(ex, 2)
    partner = {"expert": z * 2 + 1 - c}

    def z_peer(o):
        t = lax.rem(z + o, nz)
        return t, {"expert": t * 2 + c}

    def x_peer(o):
        t = lax.rem(x + o, nx)
        return t, {"dp": y * nx + t}

    def y_peer(o):
        t = lax.rem(y + o, ny)
        return t, {"dp": t * nx + x}

    def over(n, body):
        lax.fori_loop(1, n, lambda o, t: (body(o), t)[1], 0)

    def far_first(n, body):
        def one(i, t):
            body(n // 2 + (1 - 2 * lax.rem(i, 2)) * lax.div(i + 1, 2))
            return t

        lax.fori_loop(0, n - 1, one, 0)

    def remote(src, dst, s, r, device):
        return pltpu.make_async_remote_copy(
            src_ref=src, dst_ref=dst, send_sem=s, recv_sem=r, device_id=device, device_id_type=MESH
        )

    bar = pltpu.get_barrier_semaphore()

    def greet(device):
        pl.semaphore_signal(bar, inc=1, device_id=device, device_id_type=MESH)

    far_first(nz, lambda o: greet(z_peer(o)[1]))
    over(ny, lambda o: greet(y_peer(o)[1]))
    over(nx, lambda o: greet(x_peer(o)[1]))
    greet(partner)

    def cols(k):
        return pl.ds(starts[k], widths[k])

    def w_copy(k):
        return pltpu.make_async_copy(w_hbm.at[:, cols(k)], wv[k], chunk_sem.at[k, 0])

    def g_copy(k):
        return pltpu.make_async_copy(grad_hbm.at[:, cols(k)], gpair[k].at[c], chunk_sem.at[k, 1])

    def p_copy(k):
        return remote(
            grad_hbm.at[:, cols(k)], gpair[k].at[c], chunk_sem.at[k, 2], chunk_sem.at[k, 3], partner
        )

    gate_copy = pltpu.make_async_copy(gate_hbm, gate, loc_sem.at[0])
    up_copy = pltpu.make_async_copy(up_hbm, up, loc_sem.at[1])
    routes_copy = pltpu.make_async_copy(routes_hbm, routes_ref, loc_sem.at[2])
    probs_copy = pltpu.make_async_copy(probs_hbm, probs_ref, loc_sem.at[3])
    routes_copy.start()
    probs_copy.start()
    g_copy(0).start()
    gate_copy.start()
    up_copy.start()
    for k in range(1, nk):
        g_copy(k).start()
    for k in range(nk):
        w_copy(k).start()

    rgs[...] = jnp.zeros_like(rgs)
    routes_copy.wait()
    probs_copy.wait()
    named = routes_ref[...].astype(F32)
    experts = 2 * nz
    upper = (iota((tok, tok), 0) < iota((tok, tok), 1)).astype(F32).astype(BF16)
    e = iota((experts, tok), 0).astype(F32)
    hot = [(e == named[k : k + 1, :]).astype(F32) for k in range(2)]
    before = jnp.dot((hot[0] + hot[1]).astype(BF16), upper, preferred_element_type=F32)
    chip = jnp.floor(named * 0.5)
    meta[c, 0:2, :] = chip * blk
    meta[c, 2:4, :] = named - 2.0 * chip
    for k in range(2):
        meta[c, 4 + k : 5 + k, :] = jnp.sum(hot[k] * before, axis=0, keepdims=True) + (c * cap).astype(F32)
    meta[c, 6:8, :] = probs_ref[...].astype(F32)

    gate_copy.wait()
    up_copy.wait()
    for j in range(0, ff, 128):
        gv = gate[:, j : j + 128].astype(F32)
        uv = up[:, j : j + 128].astype(F32)
        sg = 1.0 / (1.0 + jnp.exp(-gv))
        av = gv * sg
        hid[:, j : j + 128] = (av * uv).astype(BF16)
        act[:, j : j + 128] = av
        slope[:, j : j + 128] = uv * (sg * (1.0 + gv * (1.0 - sg)))
    q = iota((nrow, nrow), 0)
    r = iota((nrow, nrow), 1)
    source = lax.rem(q, 2 * nz)
    slot_of = lax.div(q, 2 * nz)
    perm[...] = (r == lax.div(source, 2) * blk + lax.rem(source, 2) * cap + slot_of).astype(F32).astype(BF16)

    pl.semaphore_wait(bar, nz + ny + nx - 2)

    m_copy = remote(meta.at[c], meta.at[c], pair_sem.at[0], pair_sem.at[1], partner)
    m_copy.start()
    for k in range(nk):
        p_copy(k).start()
    m_copy.wait_recv()

    parity = c.astype(F32)
    both_halves = jnp.concatenate([meta[0], meta[1]], axis=1)
    target = jnp.where(both_halves[2:4] == parity, both_halves[0:2] + both_halves[4:6], -1.0)
    row_iota = iota((nrow, 2 * tok), 0).astype(F32)
    targets = [target[k : k + 1] for k in range(2)]
    chosen = jnp.logical_or(row_iota == targets[0], row_iota == targets[1])
    sel[...] = chosen.astype(F32).astype(BF16)
    for k in range(2):
        rows_ref[k : k + 1, :] = targets[k]

    def z_copy(k, o):
        t, device = z_peer(o)
        return remote(sent[k].at[t], arr[k].at[z], chunk_sem.at[k, 4], chunk_sem.at[k, 5], device)

    def z_all(k):
        part = arr[k].at[pl.ds(0, nz - 1)]
        return remote(part, part, chunk_sem.at[k, 4], chunk_sem.at[k, 5], partner)

    def x_copy(k, o):
        t, device = x_peer(o)
        return remote(gwb[k].at[:, t], xr[k].at[o - 1], chunk_sem.at[k, 6], chunk_sem.at[k, 7], device)

    def x_all(k):
        return remote(xr[k], xr[k], chunk_sem.at[k, 6], chunk_sem.at[k, 7], partner)

    def y_copy(k, o):
        t, device = y_peer(o)
        return remote(ys[k].at[t], yr[k].at[o - 1], chunk_sem.at[k, 8], chunk_sem.at[k, 9], device)

    def y_all(k):
        return remote(yr[k], yr[k], chunk_sem.at[k, 8], chunk_sem.at[k, 9], partner)

    def q_copy(o):
        t, device = z_peer(o)
        return remote(prow.at[t], parr.at[z], back_sem.at[0], back_sem.at[1], device)

    def s_copy(o):
        t, device = z_peer(o)
        return remote(sback.at[t], sarr.at[z], back_sem.at[2], back_sem.at[3], device)

    def q_all():
        part = parr.at[pl.ds(0, nz - 1)]
        return remote(part, part, back_sem.at[0], back_sem.at[1], partner)

    def s_all():
        part = sarr.at[pl.ds(0, nz - 1)]
        return remote(part, part, back_sem.at[2], back_sem.at[3], partner)

    def dispatch(k):
        g_copy(k).wait()
        p_copy(k).wait_recv()
        both = gpair[k][...].reshape(2 * tok, widths[k])
        picked = jnp.dot(sel[...], both, preferred_element_type=F32).astype(BF16)
        sent[k][...] = picked.reshape(nz, blk, widths[k])
        far_first(nz, lambda o: z_copy(k, o).start())
        arr[k][z] = sent[k][z]

    def combine(k):
        z_all(k).wait_recv()
        got = arr[k][...].reshape(nrow, widths[k])
        ordered = jnp.dot(perm[...], got, preferred_element_type=F32).astype(BF16)
        w_copy(k).wait()
        panel = jnp.dot(hpt[...], ordered, preferred_element_type=F32).astype(BF16)
        gwb[k][...] = panel.reshape(gwb[k].shape)
        far_first(nx, lambda o: x_copy(k, o).start())
        part = nt_dot(ordered, wv[k][...])
        if k == 0:
            u_ref[...] = part
        else:
            u_ref[...] += part

    def x_sum(k):
        x_all(k).wait_recv()
        total = gwb[k][:, x].astype(F32)
        for o in range(nx - 1):
            total = total + xr[k][o].astype(F32)
        ys[k][...] = total.astype(BF16)
        far_first(ny, lambda o: y_copy(k, o).start())

    def y_sum(k):
        y_all(k).wait_recv()
        total = ys[k][y].astype(F32)
        for o in range(ny - 1):
            total = total + yr[k][o].astype(F32)
        gw_ref[:, cols(k)] = total

    dispatch(0)

    table = None
    for k in range(2):
        prob = both_halves[6 + k : 7 + k]
        chip = jnp.floor((targets[k] + 0.5) * (1.0 / blk))
        lane = targets[k] - chip * blk
        by_chip = jnp.where(iota((nz, 2 * tok), 0).astype(F32) == chip, prob, 0.0).astype(BF16)
        by_lane = (iota((128, 2 * tok), 0).astype(F32) == lane).astype(F32).astype(BF16)
        part = nt_dot(by_chip, by_lane)
        table = part if table is None else table + part
    prow[...] = table.reshape(nz, 1, 128)
    far_first(nz, lambda o: q_copy(o).start())
    parr[z] = prow[z]
    for k in range(1, AHEAD):
        dispatch(k)

    q_all().wait_recv()
    qz = lax.div(lax.rem(iota((nrow, nz), 0), 2 * nz), 2)
    pick_chip = (qz == iota((nrow, nz), 1)).astype(F32).astype(BF16)
    ql = iota((nrow, 128), 0)
    lane_of = lax.rem(ql, 2) * cap + lax.div(ql, 2 * nz)
    own_lane = (lane_of == iota((nrow, 128), 1)).astype(F32)
    spread = jnp.dot(pick_chip, parr[...].reshape(nz, 128).astype(BF16), preferred_element_type=F32)
    weight = jnp.sum(spread * own_lane, axis=1, keepdims=True)
    for j in range(0, ff, 128):
        hp = hid[:, j : j + 128].astype(F32) * weight
        hpt[j : j + 128, :] = hp.T.astype(BF16)
        act[:, j : j + 128] = act[:, j : j + 128] * weight
        slope[:, j : j + 128] = slope[:, j : j + 128] * weight

    for k in range(nk):
        if k + AHEAD < nk:
            dispatch(k + AHEAD)
        combine(k)
        if k >= 1 and k < nk - 1:
            x_sum(k - 1)
        if k >= 2 and k < nk - 1:
            y_sum(k - 2)

    sgrad = jnp.zeros((nrow, 1), F32)
    for j in range(0, ff, 128):
        sgrad = sgrad + jnp.sum(
            hid[:, j : j + 128].astype(F32) * u_ref[:, j : j + 128], axis=1, keepdims=True
        )
    to_chip = (
        lax.div(lax.rem(iota((nz, nrow), 1), 2 * nz), 2) == iota((nz, nrow), 0)
    ).astype(F32)
    back = jnp.dot(
        to_chip, own_lane * sgrad, preferred_element_type=F32, precision=lax.Precision.HIGHEST
    )
    sback[...] = back.reshape(nz, 1, 128)
    far_first(nz, lambda o: s_copy(o).start())
    sarr[z] = sback[z]

    if nk >= 2:
        x_sum(nk - 2)
    if nk >= 3:
        y_sum(nk - 3)
    x_sum(nk - 1)

    for j in range(0, ff, 128):
        uv = u_ref[:, j : j + 128]
        gg_out[:, j : j + 128] = (uv * slope[:, j : j + 128]).astype(BF16)
        gu_out[:, j : j + 128] = (uv * act[:, j : j + 128]).astype(BF16)
    if nk >= 2:
        y_sum(nk - 2)

    masks = []
    for k in range(2):
        row = rows_ref[k : k + 1, :]
        chip = jnp.floor((row + 0.5) * (1.0 / blk))
        lane = row - chip * blk
        masks.append(
            (
                (iota((128, 2 * tok), 0).astype(F32) == lane).astype(F32),
                iota((nz, 2 * tok), 0).astype(F32) == chip,
            )
        )
    s_all().wait_recv()
    returned = sarr[...].reshape(nz, 128)
    for k in range(2):
        by_lane, mine = masks[k]
        picked = jnp.dot(
            returned, by_lane, preferred_element_type=F32, precision=lax.Precision.HIGHEST
        )
        value = jnp.sum(jnp.where(mine, picked, 0.0), axis=0, keepdims=True)
        for s in range(2):
            rgs[s, k : k + 1, :] = value[:, s * tok : (s + 1) * tok]
    r_copy = remote(rgs.at[1 - c], rgx, pair_sem.at[2], pair_sem.at[3], partner)
    r_copy.start()

    m_copy.wait_send()
    q_all().wait_send()
    s_all().wait_send()
    for k in range(nk):
        p_copy(k).wait_send()
        z_all(k).wait_send()
        x_all(k).wait_send()
    for k in range(nk - 1):
        y_all(k).wait_send()
    r_copy.wait_recv()
    rg_ref[...] = rgs[c][0:2, :] + rgx[0:2, :]
    r_copy.wait_send()
    y_sum(nk - 1)
    y_all(nk - 1).wait_send()


def write_out(n, *refs):
    ins, outs, sem = refs[:n], refs[n : 2 * n], refs[2 * n]
    copies = [pltpu.make_async_copy(ins[i], outs[i], sem.at[i]) for i in range(n)]
    for copy in copies:
        copy.start()
    for copy in copies:
        copy.wait()


def shards(nx, ny, nz, grad_out, probs, routes, saved_gate, saved_up, w_down):
    cap, ff = saved_gate.shape[3], saved_gate.shape[4]
    tok, width = grad_out.shape
    widths = WIDTHS
    blk = 2 * cap
    nrow = nz * blk
    own = ff // (nx * ny)

    def flat(saved):
        return jnp.transpose(saved[0, 0], (1, 0, 2)).reshape(nrow, ff)

    vmem = pl.BlockSpec(memory_space=pltpu.VMEM)
    anywhere = pl.BlockSpec(memory_space=pl.ANY)
    in_hbm = pl.BlockSpec(memory_space=pltpu.HBM)
    dma = pltpu.SemaphoreType.DMA

    def per_chunk(*shape):
        return tuple(pltpu.VMEM(shape + (wide,), BF16) for wide in widths)

    shapes = (
        jax.ShapeDtypeStruct((nrow, ff), BF16),
        jax.ShapeDtypeStruct((nrow, ff), BF16),
        jax.ShapeDtypeStruct((own, width), F32),
        jax.ShapeDtypeStruct((2, tok), F32),
    )
    results = pl.pallas_call(
        functools.partial(kernel, nx, ny, nz, cap, widths),
        out_shape=shapes,
        in_specs=[in_hbm] * 6,
        out_specs=(vmem, vmem, vmem, vmem),
        scratch_shapes=[
            pltpu.VMEM((2, tok), jnp.int32),
            pltpu.VMEM((2, tok), BF16),
            pltpu.VMEM((2, 8, tok), F32),
            pltpu.VMEM((nrow, 2 * tok), BF16),
            pltpu.VMEM((nz, 1, 128), F32),
            pltpu.VMEM((nz, 1, 128), F32),
            pltpu.VMEM((8, 2 * tok), F32),
            pltpu.VMEM((nrow, ff), BF16),
            pltpu.VMEM((nrow, ff), BF16),
            pltpu.VMEM((nrow, ff), BF16),
            pltpu.VMEM((nrow, ff), F32),
            pltpu.VMEM((nrow, ff), F32),
            pltpu.VMEM((ff, nrow), BF16),
            pltpu.VMEM((nrow, nrow), BF16),
            pltpu.VMEM((nrow, ff), F32),
            pltpu.VMEM((nz, 1, 128), F32),
            pltpu.VMEM((nz, 1, 128), F32),
            pltpu.VMEM((2, 8, tok), F32),
            pltpu.VMEM((8, tok), F32),
            per_chunk(2, tok),
            per_chunk(nz, blk),
            per_chunk(nz, blk),
            per_chunk(ff),
            per_chunk(ny, nx, own),
            per_chunk(nx - 1, ny, own),
            per_chunk(ny, own),
            per_chunk(ny - 1, own),
            dma((4,)),
            dma((4,)),
            dma((len(widths), 10)),
            dma((4,)),
        ],
        compiler_params=pltpu.CompilerParams(
            collective_id=0, has_side_effects=True, vmem_limit_bytes=VMEM_LIMIT
        ),
        name="expert_backward",
    )(*[
        pltpu.with_memory_space_constraint(value, pltpu.HBM)
        for value in (routes.T, probs.T, grad_out, flat(saved_gate), flat(saved_up), w_down[0])
    ])
    gg, gu, gw, rg = pl.pallas_call(
        functools.partial(write_out, len(shapes)),
        out_shape=shapes,
        in_specs=[WRITE_IN] * len(shapes),
        out_specs=(anywhere,) * len(shapes),
        scratch_shapes=[dma((len(shapes),))],
        compiler_params=pltpu.CompilerParams(vmem_limit_bytes=4 * 1024 * 1024),
        name="write_out",
    )(*results)

    def unflat(value):
        return jnp.transpose(value.reshape(cap, 2 * nz, ff), (1, 0, 2))[None, None]

    return unflat(gg), unflat(gu), gw[None], rg.T


def solution(mesh):
    nx = X_CHIPS
    ny = mesh.shape["dp"] // nx
    nz = mesh.shape["expert"] // 2
    return jax.shard_map(
        functools.partial(shards, nx, ny, nz),
        mesh=mesh,
        in_specs=(
            P(("dp", "expert"), None),
            P(("dp", "expert"), None),
            P(("dp", "expert"), None),
            P("dp", "expert", None, None, None),
            P("dp", "expert", None, None, None),
            P("expert", None, None),
        ),
        out_specs=(
            P("dp", "expert", None, None, None),
            P("dp", "expert", None, None, None),
            P("expert", "dp", None),
            P(("dp", "expert"), None),
        ),
        check_vma=False,
    )
```
